32 devices in a mesh: rep: 2 (over x), shard: 16 (over z, y, core).
Axes of the slice: x: 2, y: 2, z: 4, core: 2. Of those that a mesh axis runs over, the one named last changes fastest.
Arguments:
- features: bfloat16 [1, 2, 2048, 8192], P(None, 'rep', 'shard'), may hold values from -6 to 6
- out_grads: bfloat16 [1, 2, 2048, 1024], P(None, 'rep', 'shard'), may hold values from -6 to 6
- doc_ids: int32 [1, 2, 2048], P(None, 'rep', 'shard'), may hold values from 0 to 15, never falling along the last dimension, each value on 1 to 256 neighbouring positions
- offsets: int32 [1, 16, 128], P(None, None, 'shard'), may hold values from 0 to 15
- momentum: bfloat16 [2, 1024, 8192], P('rep', None, 'shard'), may hold values from -6 to 6
Outputs:
- residual_momentum: bfloat16 [2, 1024, 8192], P('rep', None, 'shard')
- update: bfloat16 [1, 1024, 8192], P(None, None, 'shard')
The draws below stay inside these ranges and needn't reach their ends.
Inputs may be any that keep to these rules, and one draw needn't show every extreme that they name: `doc_ids`: along each step's and group's tokens the document number never falls; every number from 0 to 15 occurs, none more than 256 times.
All inputs are finite; a program needn't handle non-finite values.
Results may differ from the reference program's by a relative error of at most 0.012.
Values may be sent and summed in bfloat16 or wider, within the bound.
A program may use at most 64 MiB of HBM per device.

```python
import math
import jax
import jax.numpy as jnp
import numpy as np
from jax import lax

D = 8192
PANEL = 1024
BLOCK = 64
STRIDE = 16
STEPS = 1
DOCS = 16
TOKENS_G = 2048
GROUPS = 2
DOC_MOST = 256


def with_ends(values, stream_key, smallest, high):
    longest = values.shape.index(max(values.shape))
    spots = []
    for shift in (0, 1):
        where = [jax.random.randint(jax.random.fold_in(stream_key, axis), (), 0, length) for axis, length in enumerate(values.shape)]
        where[longest] = (where[longest] + shift) % values.shape[longest]
        spots.append(tuple(where))
    return values.at[spots[0]].set(smallest).at[spots[1]].set(high)


def levels(own_key, dims, shards, low, top_value):
    def one(dim, shards_of):
        steps = jax.random.uniform(jax.random.fold_in(jax.random.fold_in(own_key, 6), dim), (shards_of,), jnp.float32, low / len(shards), top_value / len(shards))
        return jnp.repeat(jnp.exp(steps), dims[dim] // shards_of).reshape((-1,) + (1,) * (len(dims) - dim - 1))

    gain = one(*shards[0])
    for cut in shards[1:]:
        gain = gain * one(*cut)
    return gain


def profile(amount, total, limit, skew):
    weights = [(1 << 20) // math.isqrt(standing ** skew) + 1 for standing in range(2, amount + 1)]
    rest, holding = total - limit - (amount - 1), [1] * (amount - 1)
    while rest > 0:
        free = [i for i in range(amount - 1) if holding[i] < limit]
        pool, budget = sum([weights[i] for i in free]), rest
        for i in free:
            more = min(limit - holding[i], max(1, budget * weights[i] // pool), rest)
            holding[i] = holding[i] + more
            rest = rest - more
    return np.array([limit] + holding)


def uneven(own_key, amount, total, limit, skew):
    if amount == 2:
        one = jax.random.randint(own_key, (), max(1, total - limit), min(limit, total - 1) + 1)
        return jnp.stack([one, total - one])
    sizes = jnp.asarray(profile(amount, total, limit, skew), jnp.int32)
    pairs = (amount - 1) // 2
    giver, sink = sizes[1:1 + 2 * pairs:2], sizes[2:2 + 2 * pairs:2]
    room = jnp.minimum(giver - 1, limit - sink)
    moved = jax.random.randint(jax.random.fold_in(own_key, 1), (pairs,), 0, 1 << 20) % (room + 1)
    sizes = sizes.at[1:1 + 2 * pairs:2].set(giver - moved).at[2:2 + 2 * pairs:2].set(sink + moved)
    return sizes[jax.random.permutation(jax.random.fold_in(own_key, 2), amount)]


def noise(key, dims, scale, most, split=(), held_as=jnp.bfloat16):
    values = scale * jax.random.normal(key, dims, jnp.float32)
    if split:
        values = values * levels(key, dims, split, -0.22, 0.18)
    return jnp.clip(values, -most, most).astype(held_as)


def setup_inputs(seed: int = 0) -> dict:
    streams_of = jax.random.split(jax.random.key(seed), 6)
    features = noise(streams_of[0], (STEPS, GROUPS, TOKENS_G, D), 1.0, 6.0, ((1, 2), (2, 16)))
    out_grads = noise(streams_of[1], (STEPS, GROUPS, TOKENS_G, PANEL), 1.0, 6.0, ((1, 2), (2, 16)))
    doc_ids = jax.vmap(lambda own: jnp.searchsorted(jnp.cumsum(uneven(own, DOCS, TOKENS_G, DOC_MOST, 0)), jnp.arange(TOKENS_G), side="right"))(jax.random.split(streams_of[2], STEPS * GROUPS)).reshape((STEPS, GROUPS, TOKENS_G)).astype(jnp.int32)
    offsets = with_ends(jax.random.randint(streams_of[3], (STEPS, PANEL // BLOCK, D // BLOCK), 0, STRIDE), jax.random.fold_in(streams_of[3], 1), 0, STRIDE - 1).astype(jnp.int32)
    momentum = noise(streams_of[4], (GROUPS, PANEL, D), 1.0, 6.0, ((0, 2), (2, 16)))
    return {"features": features, "out_grads": out_grads, "doc_ids": doc_ids, "offsets": offsets, "momentum": momentum}


BETA = 0.9
CLIP = 2.0
EPS = 1e-06
PRECISE = lax.Precision.HIGHEST

def dct_table(size):
    freq = lax.broadcasted_iota(jnp.float32, (size, size), 0)
    place = lax.broadcasted_iota(jnp.float32, (size, size), 1)
    matrix = jnp.cos(math.pi * (2.0 * place + 1.0) * freq / (2.0 * size)) * math.sqrt(2.0 / size)
    return jnp.where(freq == 0, matrix / math.sqrt(2.0), matrix)

def forward(moment, matrix):
    blocks = moment.reshape(PANEL // BLOCK, BLOCK, D // BLOCK, BLOCK)
    spectrum = jnp.einsum('ku,aubv,lv->akbl', matrix, blocks, matrix, precision=PRECISE)
    return spectrum.reshape(PANEL, D)

def inverse(spectrum, matrix):
    blocks = spectrum.reshape(PANEL // BLOCK, BLOCK, D // BLOCK, BLOCK)
    spatial = jnp.einsum('ku,akbl,lv->aubv', matrix, blocks, matrix, precision=PRECISE)
    return spatial.reshape(PANEL, D)

def selector_for(offsets_step):
    grouped = jnp.repeat(offsets_step, BLOCK // STRIDE, axis=1)
    row_index = jnp.arange(BLOCK, dtype=jnp.int32)
    shift_amount = (grouped[:, None, :] - row_index[None, :, None]) % STRIDE
    residue = jnp.arange(STRIDE, dtype=jnp.int32)
    return (residue == shift_amount[..., None]).astype(jnp.float32)

def pack_entries(spectrum, selector):
    shaped = spectrum.reshape(PANEL // BLOCK, BLOCK, D // STRIDE, STRIDE)
    return lax.optimization_barrier(jnp.sum(shaped * selector, axis=-1))

def place_entries(packed, selector):
    return (packed[..., None] * selector).reshape(PANEL, D)

def expand_scale(block_scale):
    return jnp.repeat(block_scale.astype(jnp.float32), BLOCK // STRIDE, axis=-1)[..., None, :]

def compress(packed):
    shaped = packed.reshape(PANEL // BLOCK, BLOCK, D // BLOCK, BLOCK // STRIDE)
    mean_square = lax.optimization_barrier(jnp.mean(shaped * shaped, axis=(1, 3)))
    block_scale = (CLIP * jnp.sqrt(mean_square + EPS)).astype(jnp.bfloat16)
    spread = expand_scale(block_scale)
    quantized = jnp.clip(packed / spread, -1.0, 1.0).astype(jnp.bfloat16)
    return quantized.astype(jnp.float32) * spread

def reference(features, out_grads, doc_ids, offsets, momentum):
    matrix = dct_table(BLOCK)
    selectors = [selector_for(offsets[index]) for index in range(STEPS)]

    def one_group(inputs):
        group_rows, group_grads, group_ids, start_moment = inputs
        moment = start_moment.astype(jnp.float32)
        decoded_steps = []
        for index in range(STEPS):
            onehot = (group_ids[index][:, None] == jnp.arange(DOCS, dtype=jnp.int32)[None, :]).astype(jnp.float32)
            lengths = lax.optimization_barrier(jnp.sum(onehot, axis=0))
            token_weight = lax.optimization_barrier(jnp.sum(onehot / lengths[None, :], axis=1))
            scaled = (group_grads[index].astype(jnp.float32) * token_weight[:, None]).astype(jnp.bfloat16)
            gradient = lax.dot_general(scaled, group_rows[index], (((0,), (0,)), ((), ())), preferred_element_type=jnp.float32).astype(jnp.bfloat16)
            moment = BETA * moment + gradient.astype(jnp.float32)
            spectrum = forward(moment, matrix)
            packed = pack_entries(spectrum, selectors[index])
            decoded = compress(packed)
            moment = moment - inverse(place_entries(decoded, selectors[index]), matrix)
            decoded_steps.append(decoded)
        return (moment.astype(jnp.bfloat16), jnp.stack(decoded_steps))
    residual_momentum, decoded_all = lax.map(one_group, (jnp.moveaxis(features, 1, 0), jnp.moveaxis(out_grads, 1, 0), jnp.moveaxis(doc_ids, 1, 0), momentum))
    average = lax.optimization_barrier(jnp.sum(decoded_all, axis=0)) / GROUPS
    update = jnp.stack([inverse(place_entries(average[index], selectors[index]), matrix).astype(jnp.bfloat16) for index in range(STEPS)])
    return (residual_momentum, update)
```

```python
import functools
import math

import jax
import jax.numpy as jnp
import numpy as np
from jax import lax
from jax.experimental import pallas as pl
from jax.experimental.pallas import tpu as pltpu
from jax.sharding import PartitionSpec as P

BLOCK = 64
STRIDE = 16
DOCS = 16
LANES = 128

BETA = 0.9
CLIP = 2.0
EPS = 1e-06
MESH = pl.DeviceIdType.MESH
PRECISE = lax.Precision.HIGHEST


def dct_tables():
    freq = np.arange(BLOCK, dtype=np.float64)[:, None]
    place = np.arange(BLOCK, dtype=np.float64)[None, :]
    matrix = np.cos(math.pi * (2.0 * place + 1.0) * freq / (2.0 * BLOCK)) * math.sqrt(2.0 / BLOCK)
    matrix[0] /= math.sqrt(2.0)
    pair = np.kron(np.eye(LANES // BLOCK), matrix).astype(np.float32)
    high = pair.astype(jnp.bfloat16)
    low = (pair - high.astype(np.float32)).astype(jnp.bfloat16)
    return np.stack([high, low, high.T, low.T])


def split(x):
    high = x.astype(jnp.bfloat16)
    return high, (x - high.astype(jnp.float32)).astype(jnp.bfloat16)


def dot32(a, b):
    return jnp.dot(a, b, preferred_element_type=jnp.float32)


def dot3(a, b):
    return dot32(a[0], b[0]) + (dot32(a[0], b[1]) + dot32(a[1], b[0]))


def kernel(
    n, reps, feat, grads, ids, offsets, momentum, tables, res_out, upd_out,
    cols_in, grads_in, grads_t, ids_in, weights, mom_in, tab, moment, dec, dec_in, res_buf, upd_buf,
    loc_sem, ids_send, ids_recv, g_send, g_recv, f_send, f_recv, d_send, d_recv, o_sem,
):
    me = lax.axis_index("shard")
    my_rep = lax.axis_index("rep")
    chunks, _, width = cols_in.shape
    tokens = feat.shape[0]
    panel = grads.shape[1]
    row_width = chunks * width
    cores = 2 if n % 2 == 0 else 1
    sides = 2 if n % 4 == 0 else 1
    depth = n // (cores * sides)
    c = lax.rem(me, cores)
    y = lax.rem(lax.div(me, cores), sides)
    z = lax.div(me, cores * sides)

    def index(zz, yy, cc):
        return (zz * sides + yy) * cores + cc

    def token_rows(j):
        return pl.ds(pl.multiple_of(j * tokens, tokens), tokens)

    barrier = pltpu.get_barrier_semaphore()

    def greet(d, carry):
        pl.semaphore_signal(
            barrier, inc=1, device_id={"shard": lax.rem(me + d, n)}, device_id_type=MESH
        )
        return carry

    def greet_rep(d, carry):
        pl.semaphore_signal(
            barrier, inc=1, device_id={"rep": lax.rem(my_rep + d, reps)}, device_id_type=MESH
        )
        return carry

    lax.fori_loop(1, n, greet, 0)
    lax.fori_loop(1, reps, greet_rep, 0)

    local = [
        pltpu.make_async_copy(grads, grads_in.at[token_rows(me)], loc_sem.at[0]),
        pltpu.make_async_copy(ids, ids_in.at[me], loc_sem.at[1]),
        pltpu.make_async_copy(momentum, mom_in, loc_sem.at[2]),
        pltpu.make_async_copy(tables, tab, loc_sem.at[3]),
    ]
    for q in range(chunks):
        local.append(
            pltpu.make_async_copy(
                feat.at[:, pl.ds(pl.multiple_of(me * row_width + q * width, width), width)],
                cols_in.at[q, token_rows(me)],
                loc_sem.at[4 + q],
            )
        )
    for copy in local:
        copy.start()
    pl.semaphore_wait(barrier, n - 1 + reps - 1)

    def ids_copy(d):
        return pltpu.make_async_remote_copy(
            ids, ids_in.at[me], ids_send.at[d], ids_recv.at[me],
            device_id={"shard": lax.rem(me + d, n)}, device_id_type=MESH,
        )

    def grad_copy(j, slot, target, own=False):
        return pltpu.make_async_remote_copy(
            grads if own else grads_in.at[token_rows(j)],
            grads_in.at[token_rows(j)],
            g_send.at[j, slot],
            g_recv.at[j],
            device_id={"shard": target},
            device_id_type=MESH,
        )

    def feat_copy(q, d):
        target = lax.rem(me + d, n)
        start = pl.multiple_of(target * row_width + q * width, width)
        return pltpu.make_async_remote_copy(
            feat.at[:, pl.ds(start, width)],
            cols_in.at[q, token_rows(me)],
            f_send.at[q, d],
            f_recv.at[q, me],
            device_id={"shard": target},
            device_id_type=MESH,
        )

    def start_ids(d, carry):
        ids_copy(d).start()
        return carry

    lax.fori_loop(1, n, start_ids, 0)

    sends = []

    def send(condition, j, slot, target, own=False):
        sends.append((condition, j, slot, target, own))

        @pl.when(condition)
        def _():
            grad_copy(j, slot, target, own).start()

    def send_features(q):
        def step(d, carry):
            feat_copy(q, d).start()
            return carry

        lax.fori_loop(1, n, step, 0)

    def wait_grad(j):
        grad_copy(j, 0, lax.rem(me + 1, n)).wait_recv()

    always = me >= 0
    send(z + 1 < depth, me, 0, index(lax.rem(z + 1, depth), y, c), True)
    send(z >= 1, me, 1, index(lax.rem(z + depth - 1, depth), y, c), True)
    if sides > 1:
        send(always, me, 2, index(z, 1 - y, c), True)
    if cores > 1:
        send(always, me, 3, index(z, y, 1 - c), True)
    send_features(0)

    def from_side(s):
        if sides == 1:
            return
        for sign in (-1, 1) if s else (1,):
            zz = z + sign * s
            inside = (zz >= 0) & (zz < depth)
            j = index(lax.rem(zz + depth, depth), 1 - y, c)

            @pl.when(inside)
            def _():
                wait_grad(j)

            if cores > 1:
                send(inside, j, 3, index(z, y, 1 - c))

    sent = 1
    for s in range(1, depth):
        for sign in (-1, 1):
            zz = z + sign * s
            inside = (zz >= 0) & (zz < depth)
            j = index(lax.rem(zz + depth, depth), y, c)

            @pl.when(inside)
            def _():
                wait_grad(j)

            following = z - sign
            send(
                inside & (following >= 0) & (following < depth), j, 0,
                index(lax.rem(following + depth, depth), y, c),
            )
            if sides > 1:
                send(inside, j, 2, index(z, 1 - y, c))
            if cores > 1:
                send(inside, j, 3, index(z, y, 1 - c))
        from_side(s - 1)
        if sent < chunks:
            send_features(sent)
            sent += 1
    from_side(depth - 1)
    for q in range(sent, chunks):
        send_features(q)

    for copy in local:
        copy.wait()

    def wait_ids(d, carry):
        source = lax.rem(me + d, n)
        pltpu.make_async_remote_copy(
            ids, ids_in.at[source], ids_send.at[d], ids_recv.at[source],
            device_id={"shard": source}, device_id_type=MESH,
        ).wait_recv()
        return carry

    lax.fori_loop(1, n, wait_ids, 0)
    all_ids = ids_in[...]
    weight = jnp.zeros(all_ids.shape, jnp.float32)
    for doc in range(DOCS):
        hit = (all_ids == doc).astype(jnp.float32)
        count = jnp.sum(jnp.sum(hit, axis=2, keepdims=True), axis=0, keepdims=True)
        weight = weight + hit / jnp.maximum(count, 1.0)
    weights[...] = weight

    def turn(i, carry):
        group = lax.div(i, cores * (n // cores) // cores)
        j = i if cores == 1 else lax.rem(i, n // cores) * cores + lax.rem(c + group, cores)

        @pl.when(i >= n // cores)
        def _():
            wait_grad(j)

        row = weights[j]
        for first in range(0, panel, LANES):
            part = grads_in[token_rows(j), first : first + LANES].astype(jnp.float32)
            grads_t[first : first + LANES, token_rows(j)] = (part.T * row).astype(jnp.bfloat16)
        return carry

    lax.fori_loop(0, n, turn, 0)

    forward_pair = (tab[0], tab[1])
    inverse_pair = (tab[2], tab[3])
    folds = panel // STRIDE
    per_tile = LANES // STRIDE
    tall = BLOCK // STRIDE
    tiles = panel // LANES
    row_sum = (
        lax.broadcasted_iota(jnp.int32, (folds, folds), 0) // tall
        == lax.broadcasted_iota(jnp.int32, (folds, folds), 1) // tall
    ).astype(jnp.float32)
    lane_sum = (
        lax.broadcasted_iota(jnp.int32, (width, width), 0) // BLOCK
        == lax.broadcasted_iota(jnp.int32, (width, width), 1) // BLOCK
    ).astype(jnp.float32)
    residue = (
        lax.broadcasted_iota(jnp.int32, (STRIDE, width), 0)
        + lax.broadcasted_iota(jnp.int32, (STRIDE, width), 1)
    ) % STRIDE

    def mask_of(q, tile):
        rows = []
        for a in range(tile * LANES // BLOCK, (tile + 1) * LANES // BLOCK):
            hit = residue == offsets[q, a : a + 1, :]
            rows += [hit.astype(jnp.float32)] * tall
        return jnp.concatenate(rows, axis=0)

    def spread(values, mask):
        tall_values = jnp.broadcast_to(values[:, None, :], (per_tile, STRIDE, width))
        return tall_values.reshape(LANES, width) * mask

    def invert(values, mask):
        mixed = dot3(inverse_pair, split(spread(values, mask)))
        return dot3(split(mixed), forward_pair)

    def out_copy(q, which):
        return pltpu.make_async_copy(
            (res_buf, upd_buf)[which].at[q],
            (res_out, upd_out)[which].at[:, pl.ds(pl.multiple_of(q * width, width), width)],
            o_sem.at[which, q],
        )

    def dec_copy(q, d):
        return pltpu.make_async_remote_copy(
            dec.at[q], dec_in.at[q, my_rep], d_send.at[q, d], d_recv.at[q, my_rep],
            device_id={"rep": lax.rem(my_rep + d, reps)}, device_id_type=MESH,
        )

    def first_half(q, carry):
        def wait_feat(d, inner):
            source = lax.rem(me + d, n)
            pltpu.make_async_remote_copy(
                feat.at[:, pl.ds(0, width)], cols_in.at[q, token_rows(source)],
                f_send.at[q, d], f_recv.at[q, source],
                device_id={"shard": source}, device_id_type=MESH,
            ).wait_recv()
            return inner

        lax.fori_loop(1, n, wait_feat, 0)
        lanes = pl.ds(pl.multiple_of(q * width, width), width)
        folded = []
        for tile in range(tiles):
            rows = slice(tile * LANES, (tile + 1) * LANES)
            gradient = dot32(grads_t[rows, :], cols_in[q]).astype(jnp.bfloat16).astype(jnp.float32)
            mom = BETA * mom_in[rows, lanes].astype(jnp.float32) + gradient
            moment[rows, :] = mom
            mixed = dot3(forward_pair, split(mom))
            spectrum = dot3(split(mixed), inverse_pair)
            chosen = (spectrum * mask_of(q, tile)).reshape(per_tile, STRIDE, width)
            folded.append(jnp.sum(chosen, axis=1))
        packed = jnp.concatenate(folded, axis=0)
        total = jnp.dot(row_sum, packed * packed, precision=PRECISE, preferred_element_type=jnp.float32)
        total = jnp.dot(total, lane_sum, precision=PRECISE, preferred_element_type=jnp.float32)
        mean_square = total / (BLOCK * tall)
        scale = (CLIP * jnp.sqrt(mean_square + EPS)).astype(jnp.bfloat16).astype(jnp.float32)
        quantized = jnp.clip(packed / scale, -1.0, 1.0).astype(jnp.bfloat16)
        decoded = quantized.astype(jnp.float32) * scale
        dec[q] = decoded

        def start_dec(d, inner):
            dec_copy(q, d).start()
            return inner

        lax.fori_loop(1, reps, start_dec, 0)
        for tile in range(tiles):
            rows = slice(tile * LANES, (tile + 1) * LANES)
            part = decoded[tile * per_tile : (tile + 1) * per_tile]
            back = invert(part, mask_of(q, tile))
            res_buf[q, rows, :] = (moment[rows, :] - back).astype(jnp.bfloat16)
        out_copy(q, 0).start()

        def wait_dec(d, inner):
            source = lax.rem(my_rep + d, reps)
            pltpu.make_async_remote_copy(
                dec.at[q], dec_in.at[q, source], d_send.at[q, d], d_recv.at[q, source],
                device_id={"rep": source}, device_id_type=MESH,
            ).wait_recv()
            return inner + dec_in[q, source]

        average = lax.fori_loop(1, reps, wait_dec, decoded) / reps
        for tile in range(tiles):
            rows = slice(tile * LANES, (tile + 1) * LANES)
            part = average[tile * per_tile : (tile + 1) * per_tile]
            upd_buf[q, rows, :] = invert(part, mask_of(q, tile)).astype(jnp.bfloat16)
        out_copy(q, 1).start()
        return carry

    lax.fori_loop(0, chunks, first_half, 0)

    def drain(q, carry):
        def sent_feat(d, inner):
            feat_copy(q, d).wait_send()
            return inner

        def sent_dec(d, inner):
            dec_copy(q, d).wait_send()
            return inner

        lax.fori_loop(1, n, sent_feat, 0)
        lax.fori_loop(1, reps, sent_dec, 0)
        out_copy(q, 0).wait()
        out_copy(q, 1).wait()
        return carry

    def sent_ids(d, carry):
        ids_copy(d).wait_send()
        return carry

    lax.fori_loop(1, n, sent_ids, 0)
    for condition, j, slot, target, own in sends:

        @pl.when(condition)
        def _():
            grad_copy(j, slot, target, own).wait_send()

    lax.fori_loop(0, chunks, drain, 0)


def body(n, reps, features, out_grads, doc_ids, offsets, momentum):
    feat = features[0, 0]
    grads = out_grads[0, 0]
    tokens, model = feat.shape
    panel = grads.shape[1]
    row_width = momentum.shape[2]
    width = LANES
    chunks = row_width // width
    wide = jnp.repeat(offsets[0], BLOCK, axis=1).reshape(panel // BLOCK, chunks, width)
    wide = jnp.transpose(wide, (1, 0, 2))
    folds = panel // STRIDE
    anywhere = pl.BlockSpec(memory_space=pl.ANY)
    vmem = pl.BlockSpec(memory_space=pltpu.VMEM)
    dma = pltpu.SemaphoreType.DMA
    residual, update = pl.pallas_call(
        functools.partial(kernel, n, reps),
        out_shape=(
            jax.ShapeDtypeStruct((panel, row_width), jnp.bfloat16),
            jax.ShapeDtypeStruct((panel, row_width), jnp.bfloat16),
        ),
        in_specs=[anywhere, anywhere, vmem, vmem, anywhere, anywhere],
        out_specs=(anywhere, anywhere),
        scratch_shapes=[
            pltpu.VMEM((chunks, n * tokens, width), jnp.bfloat16),
            pltpu.VMEM((n * tokens, panel), jnp.bfloat16),
            pltpu.VMEM((panel, n * tokens), jnp.bfloat16),
            pltpu.VMEM((n, 1, tokens), jnp.int32),
            pltpu.VMEM((n, 1, tokens), jnp.float32),
            pltpu.VMEM((panel, row_width), jnp.bfloat16),
            pltpu.VMEM((4, LANES, LANES), jnp.bfloat16),
            pltpu.VMEM((panel, width), jnp.float32),
            pltpu.VMEM((chunks, folds, width), jnp.float32),
            pltpu.VMEM((chunks, reps, folds, width), jnp.float32),
            pltpu.VMEM((chunks, panel, width), jnp.bfloat16),
            pltpu.VMEM((chunks, panel, width), jnp.bfloat16),
            dma((4 + chunks,)),
            dma((n,)),
            dma((n,)),
            dma((n, 4)),
            dma((n,)),
            dma((chunks, n)),
            dma((chunks, n)),
            dma((chunks, reps)),
            dma((chunks, reps)),
            dma((2, chunks)),
        ],
        compiler_params=pltpu.CompilerParams(collective_id=0, has_side_effects=True),
    )(feat, grads, doc_ids[0], wide, momentum[0], jnp.asarray(dct_tables()))
    return residual[None], update[None]


def solution(mesh):
    return jax.shard_map(
        functools.partial(body, mesh.shape["shard"], mesh.shape["rep"]),
        mesh=mesh,
        in_specs=(
            P(None, "rep", "shard", None),
            P(None, "rep", "shard", None),
            P(None, "rep", "shard"),
            P(None, None, "shard"),
            P("rep", None, "shard"),
        ),
        out_specs=(P("rep", None, "shard"), P(None, None, "shard")),
        check_vma=False,
    )
```

```python
import functools
import math

import jax
import jax.numpy as jnp
import numpy as np
from jax import lax
from jax.experimental import pallas as pl
from jax.experimental.pallas import tpu as pltpu
from jax.sharding import PartitionSpec as P

BLOCK = 64
STRIDE = 16
DOCS = 16
LANES = 128

BETA = 0.9
CLIP = 2.0
EPS = 1e-06
MESH = pl.DeviceIdType.MESH
PRECISE = lax.Precision.HIGHEST


def dct_tables():
    freq = np.arange(BLOCK, dtype=np.float64)[:, None]
    place = np.arange(BLOCK, dtype=np.float64)[None, :]
    matrix = np.cos(math.pi * (2.0 * place + 1.0) * freq / (2.0 * BLOCK)) * math.sqrt(2.0 / BLOCK)
    matrix[0] /= math.sqrt(2.0)
    pair = np.kron(np.eye(LANES // BLOCK), matrix).astype(np.float32)
    high = pair.astype(jnp.bfloat16)
    low = (pair - high.astype(np.float32)).astype(jnp.bfloat16)
    zero = np.zeros_like(high)
    left = [np.concatenate([high, low]), np.concatenate([high.T, low.T])]
    right = [np.block([[high.T, low.T], [high.T, zero]]), np.block([[high, low], [high, zero]])]
    return np.stack(left), np.stack(right)


def split(x):
    high = x.astype(jnp.bfloat16)
    return high, (x - high.astype(jnp.float32)).astype(jnp.bfloat16)


def dot32(a, b):
    return jnp.dot(a, b, preferred_element_type=jnp.float32)


def kernel(
    n, reps, feat, grads, ids, offsets, momentum, left, right, res_out, upd_out,
    cols_in, grads_in, grads_t, ids_in, weights, mom_in, tab_l, tab_r, wide, moment, mix, dec, dec_in, res_buf, upd_buf,
    loc_sem, ids_send, ids_recv, g_send, g_recv, f_send, f_recv, d_send, d_recv, o_sem,
):
    me = lax.axis_index("shard")
    my_rep = lax.axis_index("rep")
    chunks, _, width = cols_in.shape
    tokens = feat.shape[0]
    panel = grads.shape[1]
    row_width = chunks * width
    cores = 2 if n % 2 == 0 else 1
    sides = 2 if n % 4 == 0 else 1
    depth = n // (cores * sides)
    c = lax.rem(me, cores)
    y = lax.rem(lax.div(me, cores), sides)
    z = lax.div(me, cores * sides)

    def index(zz, yy, cc):
        return (zz * sides + yy) * cores + cc

    def token_rows(j):
        return pl.ds(pl.multiple_of(j * tokens, tokens), tokens)

    barrier = pltpu.get_barrier_semaphore()

    def greet(d, carry):
        pl.semaphore_signal(
            barrier, inc=1, device_id={"shard": lax.rem(me + d, n)}, device_id_type=MESH
        )
        return carry

    def greet_rep(d, carry):
        pl.semaphore_signal(
            barrier, inc=1, device_id={"rep": lax.rem(my_rep + d, reps)}, device_id_type=MESH
        )
        return carry

    lax.fori_loop(1, n, greet, 0)
    lax.fori_loop(1, reps, greet_rep, 0)

    local = [
        pltpu.make_async_copy(grads, grads_in.at[token_rows(me)], loc_sem.at[0]),
        pltpu.make_async_copy(ids, ids_in.at[me], loc_sem.at[1]),
        pltpu.make_async_copy(momentum, mom_in, loc_sem.at[2]),
        pltpu.make_async_copy(left, tab_l, loc_sem.at[3]),
        pltpu.make_async_copy(right, tab_r, loc_sem.at[4]),
    ]
    for q in range(chunks):
        local.append(
            pltpu.make_async_copy(
                feat.at[:, pl.ds(pl.multiple_of(me * row_width + q * width, width), width)],
                cols_in.at[q, token_rows(me)],
                loc_sem.at[5 + q],
            )
        )
    for copy in local:
        copy.start()
    pl.semaphore_wait(barrier, n - 1 + reps - 1)

    def ids_copy(d):
        return pltpu.make_async_remote_copy(
            ids, ids_in.at[me], ids_send.at[d], ids_recv.at[me],
            device_id={"shard": lax.rem(me + d, n)}, device_id_type=MESH,
        )

    def grad_copy(j, slot, target, own=False):
        return pltpu.make_async_remote_copy(
            grads if own else grads_in.at[token_rows(j)],
            grads_in.at[token_rows(j)],
            g_send.at[j, slot],
            g_recv.at[j],
            device_id={"shard": target},
            device_id_type=MESH,
        )

    def feat_copy(q, d):
        target = lax.rem(me + d, n)
        start = pl.multiple_of(target * row_width + q * width, width)
        return pltpu.make_async_remote_copy(
            feat.at[:, pl.ds(start, width)],
            cols_in.at[q, token_rows(me)],
            f_send.at[q, d],
            f_recv.at[q, me],
            device_id={"shard": target},
            device_id_type=MESH,
        )

    def start_ids(d, carry):
        ids_copy(d).start()
        return carry

    lax.fori_loop(1, n, start_ids, 0)

    sends = []

    def send(condition, j, slot, target, own=False):
        sends.append((condition, j, slot, target, own))

        @pl.when(condition)
        def _():
            grad_copy(j, slot, target, own).start()

    def send_features(q):
        def step(d, carry):
            feat_copy(q, d).start()
            return carry

        lax.fori_loop(1, n, step, 0)

    def wait_grad(j):
        grad_copy(j, 0, lax.rem(me + 1, n)).wait_recv()

    always = me >= 0
    send(z + 1 < depth, me, 0, index(lax.rem(z + 1, depth), y, c), True)
    send(z >= 1, me, 1, index(lax.rem(z + depth - 1, depth), y, c), True)
    if sides > 1:
        send(always, me, 2, index(z, 1 - y, c), True)
    if cores > 1:
        send(always, me, 3, index(z, y, 1 - c), True)
    def from_side(s):
        if sides == 1:
            return
        for sign in (-1, 1) if s else (1,):
            zz = z + sign * s
            inside = (zz >= 0) & (zz < depth)
            j = index(lax.rem(zz + depth, depth), 1 - y, c)

            @pl.when(inside)
            def _():
                wait_grad(j)

            if cores > 1:
                send(inside, j, 3, index(z, y, 1 - c))

    sent = 0
    for s in range(1, depth):
        for sign in (-1, 1):
            zz = z + sign * s
            inside = (zz >= 0) & (zz < depth)
            j = index(lax.rem(zz + depth, depth), y, c)

            @pl.when(inside)
            def _():
                wait_grad(j)

            following = z - sign
            send(
                inside & (following >= 0) & (following < depth), j, 0,
                index(lax.rem(following + depth, depth), y, c),
            )
            if sides > 1:
                send(inside, j, 2, index(z, 1 - y, c))
            if cores > 1:
                send(inside, j, 3, index(z, y, 1 - c))
        from_side(s - 1)
        for q in range(sent, min(chunks, (s >= depth // 2) + chunks * (s > depth // 2))):
            send_features(q)
            sent = q + 1
    from_side(depth - 1)
    for q in range(sent, chunks):
        send_features(q)

    own_blocks = offsets.shape[0]
    for q in range(chunks):
        block_of = (lax.broadcasted_iota(jnp.int32, (own_blocks, width), 1) + q * width) // BLOCK
        pick = (block_of == lax.broadcasted_iota(jnp.int32, (own_blocks, width), 0)).astype(jnp.float32)
        wide[q] = lax.dot_general(
            offsets[...].astype(jnp.float32), pick, (((0,), (0,)), ((), ())),
            precision=PRECISE, preferred_element_type=jnp.float32,
        ).astype(jnp.int32)

    for copy in local:
        copy.wait()

    def wait_ids(d, carry):
        source = lax.rem(me + d, n)
        pltpu.make_async_remote_copy(
            ids, ids_in.at[source], ids_send.at[d], ids_recv.at[source],
            device_id={"shard": source}, device_id_type=MESH,
        ).wait_recv()
        return carry

    lax.fori_loop(1, n, wait_ids, 0)
    all_ids = ids_in[...]
    weight = jnp.zeros(all_ids.shape, jnp.float32)
    for doc in range(DOCS):
        hit = (all_ids == doc).astype(jnp.float32)
        count = jnp.sum(jnp.sum(hit, axis=2, keepdims=True), axis=0, keepdims=True)
        weight = weight + hit / jnp.maximum(count, 1.0)
    weights[...] = weight

    def turn(i, carry):
        group = lax.div(i, cores * (n // cores) // cores)
        j = i if cores == 1 else lax.rem(i, n // cores) * cores + lax.rem(c + group, cores)

        @pl.when(i >= n // cores)
        def _():
            wait_grad(j)

        row = weights[j]
        for first in range(0, panel, LANES):
            part = grads_in[token_rows(j), first : first + LANES].astype(jnp.float32)
            grads_t[first : first + LANES, token_rows(j)] = (part.T * row).astype(jnp.bfloat16)
        return carry

    lax.fori_loop(0, n, turn, 0)

    folds = panel // STRIDE
    per_tile = LANES // STRIDE
    tall = BLOCK // STRIDE
    tiles = panel // LANES
    row_sum = (
        lax.broadcasted_iota(jnp.int32, (folds, folds), 0) // tall
        == lax.broadcasted_iota(jnp.int32, (folds, folds), 1) // tall
    ).astype(jnp.float32)
    lane_sum = (
        lax.broadcasted_iota(jnp.int32, (width, width), 0) // BLOCK
        == lax.broadcasted_iota(jnp.int32, (width, width), 1) // BLOCK
    ).astype(jnp.float32)
    residue = (
        lax.broadcasted_iota(jnp.int32, (STRIDE, width), 0)
        + lax.broadcasted_iota(jnp.int32, (STRIDE, width), 1)
    ) % STRIDE

    def mask_of(q, tile):
        rows = []
        for a in range(tile * LANES // BLOCK, (tile + 1) * LANES // BLOCK):
            hit = residue == wide[q, a : a + 1, :]
            rows += [hit.astype(jnp.float32)] * tall
        return jnp.concatenate(rows, axis=0)

    def spread(values, mask):
        tall_values = jnp.broadcast_to(values[:, None, :], (per_tile, STRIDE, width))
        return tall_values.reshape(LANES, width) * mask

    def mix_rows(tile, values, way):
        both = dot32(tab_l[way], jnp.concatenate(split(values), axis=1))
        mixed = both[:LANES, :width] + (both[:LANES, width:] + both[LANES:, :width])
        high, low = split(mixed)
        mix[tile * LANES : (tile + 1) * LANES, :width] = high
        mix[tile * LANES : (tile + 1) * LANES, width:] = low

    def mix_columns(way):
        both = dot32(mix[...], tab_r[way])
        return both[:, :width] + both[:, width:]

    def invert(q, values):
        for tile in range(tiles):
            part = values[tile * per_tile : (tile + 1) * per_tile]
            mix_rows(tile, spread(part, mask_of(q, tile)), 1)
        return mix_columns(1)

    def out_copy(q, which):
        return pltpu.make_async_copy(
            (res_buf, upd_buf)[which].at[q],
            (res_out, upd_out)[which].at[:, pl.ds(pl.multiple_of(q * width, width), width)],
            o_sem.at[which, q],
        )

    def dec_copy(q, d):
        return pltpu.make_async_remote_copy(
            dec.at[q], dec_in.at[q, my_rep], d_send.at[q, d], d_recv.at[q, my_rep],
            device_id={"rep": lax.rem(my_rep + d, reps)}, device_id_type=MESH,
        )

    def finish_update(q):
        def wait_dec(d, inner):
            source = lax.rem(my_rep + d, reps)
            pltpu.make_async_remote_copy(
                dec.at[q], dec_in.at[q, source], d_send.at[q, d], d_recv.at[q, source],
                device_id={"rep": source}, device_id_type=MESH,
            ).wait_recv()
            return inner + dec_in[q, source]

        average = lax.fori_loop(1, reps, wait_dec, dec[q]) / reps
        upd_buf[q] = invert(q, average).astype(jnp.bfloat16)
        out_copy(q, 1).start()

    def first_half(q, carry):
        def wait_feat(d, inner):
            source = lax.rem(me + d, n)
            pltpu.make_async_remote_copy(
                feat.at[:, pl.ds(0, width)], cols_in.at[q, token_rows(source)],
                f_send.at[q, d], f_recv.at[q, source],
                device_id={"shard": source}, device_id_type=MESH,
            ).wait_recv()
            return inner

        lax.fori_loop(1, n, wait_feat, 0)
        lanes = pl.ds(pl.multiple_of(q * width, width), width)
        gradient = dot32(grads_t[...], cols_in[q]).astype(jnp.bfloat16).astype(jnp.float32)
        moment[...] = BETA * mom_in[:, lanes].astype(jnp.float32) + gradient
        for tile in range(tiles):
            mix_rows(tile, moment[tile * LANES : (tile + 1) * LANES, :], 0)
        spectrum = mix_columns(0)
        folded = []
        for tile in range(tiles):
            rows = slice(tile * LANES, (tile + 1) * LANES)
            chosen = (spectrum[rows] * mask_of(q, tile)).reshape(per_tile, STRIDE, width)
            folded.append(jnp.sum(chosen, axis=1))
        packed = jnp.concatenate(folded, axis=0)
        total = jnp.dot(row_sum, packed * packed, precision=PRECISE, preferred_element_type=jnp.float32)
        total = jnp.dot(total, lane_sum, precision=PRECISE, preferred_element_type=jnp.float32)
        mean_square = total / (BLOCK * tall)
        scale = (CLIP * jnp.sqrt(mean_square + EPS)).astype(jnp.bfloat16).astype(jnp.float32)
        quantized = jnp.clip(packed / scale, -1.0, 1.0).astype(jnp.bfloat16)
        decoded = quantized.astype(jnp.float32) * scale
        dec[q] = decoded

        def start_dec(d, inner):
            dec_copy(q, d).start()
            return inner

        lax.fori_loop(1, reps, start_dec, 0)
        res_buf[q] = (moment[...] - invert(q, decoded)).astype(jnp.bfloat16)
        out_copy(q, 0).start()

        @pl.when(q > 0)
        def _():
            finish_update(q - 1)

        return carry

    lax.fori_loop(0, chunks, first_half, 0)
    finish_update(chunks - 1)

    def drain(q, carry):
        def sent_feat(d, inner):
            feat_copy(q, d).wait_send()
            return inner

        def sent_dec(d, inner):
            dec_copy(q, d).wait_send()
            return inner

        lax.fori_loop(1, n, sent_feat, 0)
        lax.fori_loop(1, reps, sent_dec, 0)
        out_copy(q, 0).wait()
        out_copy(q, 1).wait()
        return carry

    def sent_ids(d, carry):
        ids_copy(d).wait_send()
        return carry

    lax.fori_loop(1, n, sent_ids, 0)
    for condition, j, slot, target, own in sends:

        @pl.when(condition)
        def _():
            grad_copy(j, slot, target, own).wait_send()

    lax.fori_loop(0, chunks, drain, 0)


def body(n, reps, features, out_grads, doc_ids, offsets, momentum):
    feat = features[0, 0]
    grads = out_grads[0, 0]
    tokens, model = feat.shape
    panel = grads.shape[1]
    row_width = momentum.shape[2]
    width = LANES
    chunks = row_width // width
    folds = panel // STRIDE
    anywhere = pl.BlockSpec(memory_space=pl.ANY)
    vmem = pl.BlockSpec(memory_space=pltpu.VMEM)
    dma = pltpu.SemaphoreType.DMA
    residual, update = pl.pallas_call(
        functools.partial(kernel, n, reps),
        out_shape=(
            jax.ShapeDtypeStruct((panel, row_width), jnp.bfloat16),
            jax.ShapeDtypeStruct((panel, row_width), jnp.bfloat16),
        ),
        in_specs=[anywhere, anywhere, vmem, vmem, anywhere, anywhere, anywhere],
        out_specs=(anywhere, anywhere),
        scratch_shapes=[
            pltpu.VMEM((chunks, n * tokens, width), jnp.bfloat16),
            pltpu.VMEM((n * tokens, panel), jnp.bfloat16),
            pltpu.VMEM((panel, n * tokens), jnp.bfloat16),
            pltpu.VMEM((n, 1, tokens), jnp.int32),
            pltpu.VMEM((n, 1, tokens), jnp.float32),
            pltpu.VMEM((panel, row_width), jnp.bfloat16),
            pltpu.VMEM((2, 2 * LANES, LANES), jnp.bfloat16),
            pltpu.VMEM((2, 2 * LANES, 2 * width), jnp.bfloat16),
            pltpu.VMEM((chunks, panel // BLOCK, width), jnp.int32),
            pltpu.VMEM((panel, width), jnp.float32),
            pltpu.VMEM((panel, 2 * width), jnp.bfloat16),
            pltpu.VMEM((chunks, folds, width), jnp.float32),
            pltpu.VMEM((chunks, reps, folds, width), jnp.float32),
            pltpu.VMEM((chunks, panel, width), jnp.bfloat16),
            pltpu.VMEM((chunks, panel, width), jnp.bfloat16),
            dma((5 + chunks,)),
            dma((n,)),
            dma((n,)),
            dma((n, 4)),
            dma((n,)),
            dma((chunks, n)),
            dma((chunks, n)),
            dma((chunks, reps)),
            dma((chunks, reps)),
            dma((2, chunks)),
        ],
        compiler_params=pltpu.CompilerParams(collective_id=0, has_side_effects=True),
    )(feat, grads, doc_ids[0], offsets[0].T, momentum[0], *map(jnp.asarray, dct_tables()))
    return residual[None], update[None]


def solution(mesh):
    return jax.shard_map(
        functools.partial(body, mesh.shape["shard"], mesh.shape["rep"]),
        mesh=mesh,
        in_specs=(
            P(None, "rep", "shard", None),
            P(None, "rep", "shard", None),
            P(None, "rep", "shard"),
            P(None, None, "shard"),
            P("rep", None, "shard"),
        ),
        out_specs=(P("rep", None, "shard"), P(None, None, "shard")),
        check_vma=False,
    )
```

```python
import functools
import math

import jax
import jax.numpy as jnp
import numpy as np
from jax import lax
from jax.experimental import pallas as pl
from jax.experimental.pallas import tpu as pltpu
from jax.sharding import PartitionSpec as P

BLOCK = 64
STRIDE = 16
DOCS = 16
LANES = 128

BETA = 0.9
CLIP = 2.0
EPS = 1e-06
MESH = pl.DeviceIdType.MESH
PRECISE = lax.Precision.HIGHEST


def dct_tables():
    freq = np.arange(BLOCK, dtype=np.float64)[:, None]
    place = np.arange(BLOCK, dtype=np.float64)[None, :]
    matrix = np.cos(math.pi * (2.0 * place + 1.0) * freq / (2.0 * BLOCK)) * math.sqrt(2.0 / BLOCK)
    matrix[0] /= math.sqrt(2.0)
    pair = np.kron(np.eye(LANES // BLOCK), matrix).astype(np.float32)
    high = pair.astype(jnp.bfloat16)
    low = (pair - high.astype(np.float32)).astype(jnp.bfloat16)
    zero = np.zeros_like(high)
    left = [np.concatenate([high, low]), np.concatenate([high.T, low.T])]
    right = [np.block([[high.T, low.T], [high.T, zero]]), np.block([[high, low], [high, zero]])]
    return np.stack(left), np.stack(right)


def split(x):
    high = x.astype(jnp.bfloat16)
    return high, (x - high.astype(jnp.float32)).astype(jnp.bfloat16)


def dot32(a, b):
    return jnp.dot(a, b, preferred_element_type=jnp.float32)


def kernel(
    n, reps, feat, grads, ids, offsets, momentum, left, right, res_out, upd_out,
    cols_in, grads_in, grads_t, ids_in, weights, mom_in, tab_l, tab_r, wide, moment, mix, dec, dec_in, res_buf, upd_buf,
    loc_sem, ids_send, ids_recv, g_send, g_recv, f_send, f_recv, d_send, d_recv, o_sem,
):
    me = lax.axis_index("shard")
    my_rep = lax.axis_index("rep")
    chunks, _, width = cols_in.shape
    tokens = feat.shape[0]
    panel = grads.shape[1]
    row_width = chunks * width
    cores = 2 if n % 2 == 0 else 1
    sides = 2 if n % 4 == 0 else 1
    depth = n // (cores * sides)
    c = lax.rem(me, cores)
    y = lax.rem(lax.div(me, cores), sides)
    z = lax.div(me, cores * sides)

    def index(zz, yy, cc):
        return (zz * sides + yy) * cores + cc

    def token_rows(j):
        return pl.ds(pl.multiple_of(j * tokens, tokens), tokens)

    barrier = pltpu.get_barrier_semaphore()

    def greet(d, carry):
        pl.semaphore_signal(
            barrier, inc=1, device_id={"shard": lax.rem(me + d, n)}, device_id_type=MESH
        )
        return carry

    def greet_rep(d, carry):
        pl.semaphore_signal(
            barrier, inc=1, device_id={"rep": lax.rem(my_rep + d, reps)}, device_id_type=MESH
        )
        return carry

    lax.fori_loop(1, n, greet, 0)
    lax.fori_loop(1, reps, greet_rep, 0)

    local = [
        pltpu.make_async_copy(grads, grads_in.at[token_rows(me)], loc_sem.at[0]),
        pltpu.make_async_copy(ids, ids_in.at[me], loc_sem.at[1]),
        pltpu.make_async_copy(momentum, mom_in, loc_sem.at[2]),
        pltpu.make_async_copy(left, tab_l, loc_sem.at[3]),
        pltpu.make_async_copy(right, tab_r, loc_sem.at[4]),
    ]
    for q in range(chunks):
        local.append(
            pltpu.make_async_copy(
                feat.at[:, pl.ds(pl.multiple_of(me * row_width + q * width, width), width)],
                cols_in.at[q, token_rows(me)],
                loc_sem.at[5 + q],
            )
        )
    for copy in local:
        copy.start()
    pl.semaphore_wait(barrier, n - 1 + reps - 1)

    def ids_copy(d):
        return pltpu.make_async_remote_copy(
            ids, ids_in.at[me], ids_send.at[d], ids_recv.at[me],
            device_id={"shard": lax.rem(me + d, n)}, device_id_type=MESH,
        )

    def grad_copy(j, slot, target, own=False):
        return pltpu.make_async_remote_copy(
            grads if own else grads_in.at[token_rows(j)],
            grads_in.at[token_rows(j)],
            g_send.at[j, slot],
            g_recv.at[j],
            device_id={"shard": target},
            device_id_type=MESH,
        )

    def feat_copy(q, d):
        target = lax.rem(me + d, n)
        start = pl.multiple_of(target * row_width + q * width, width)
        return pltpu.make_async_remote_copy(
            feat.at[:, pl.ds(start, width)],
            cols_in.at[q, token_rows(me)],
            f_send.at[q, d],
            f_recv.at[q, me],
            device_id={"shard": target},
            device_id_type=MESH,
        )

    def start_ids(d, carry):
        ids_copy(d).start()
        return carry

    lax.fori_loop(1, n, start_ids, 0)

    sends = []

    def send(condition, j, slot, target, own=False):
        sends.append((condition, j, slot, target, own))

        @pl.when(condition)
        def _():
            grad_copy(j, slot, target, own).start()

    def send_features(q):
        def step(d, carry):
            feat_copy(q, d).start()
            return carry

        lax.fori_loop(1, n, step, 0)

    def wait_grad(j):
        grad_copy(j, 0, lax.rem(me + 1, n)).wait_recv()

    always = me >= 0
    send(z + 1 < depth, me, 0, index(lax.rem(z + 1, depth), y, c), True)
    send(z >= 1, me, 1, index(lax.rem(z + depth - 1, depth), y, c), True)
    if sides > 1:
        send(always, me, 2, index(z, 1 - y, c), True)
    if cores > 1:
        send(always, me, 3, index(z, y, 1 - c), True)
    def from_side(s):
        if sides == 1:
            return
        for sign in (-1, 1) if s else (1,):
            zz = z + sign * s
            inside = (zz >= 0) & (zz < depth)
            j = index(lax.rem(zz + depth, depth), 1 - y, c)

            @pl.when(inside)
            def _():
                wait_grad(j)

            if cores > 1:
                send(inside, j, 3, index(z, y, 1 - c))

    sent = 0
    for s in range(1, depth):
        for sign in (-1, 1):
            zz = z + sign * s
            inside = (zz >= 0) & (zz < depth)
            j = index(lax.rem(zz + depth, depth), y, c)

            @pl.when(inside)
            def _():
                wait_grad(j)

            following = z - sign
            send(
                inside & (following >= 0) & (following < depth), j, 0,
                index(lax.rem(following + depth, depth), y, c),
            )
            if sides > 1:
                send(inside, j, 2, index(z, 1 - y, c))
            if cores > 1:
                send(inside, j, 3, index(z, y, 1 - c))
        due = (chunks + 1) // 2 if s == depth // 2 else chunks if s > depth // 2 else 0
        for q in range(sent, due):
            send_features(q)
            sent = q + 1
    for s in range(depth):
        from_side(s)
    for q in range(sent, chunks):
        send_features(q)

    own_blocks = offsets.shape[0]
    for q in range(chunks):
        block_of = (lax.broadcasted_iota(jnp.int32, (own_blocks, width), 1) + q * width) // BLOCK
        pick = (block_of == lax.broadcasted_iota(jnp.int32, (own_blocks, width), 0)).astype(jnp.float32)
        wide[q] = lax.dot_general(
            offsets[...].astype(jnp.float32), pick, (((0,), (0,)), ((), ())),
            precision=PRECISE, preferred_element_type=jnp.float32,
        ).astype(jnp.int32)

    for copy in local:
        copy.wait()

    def wait_ids(d, carry):
        source = lax.rem(me + d, n)
        pltpu.make_async_remote_copy(
            ids, ids_in.at[source], ids_send.at[d], ids_recv.at[source],
            device_id={"shard": source}, device_id_type=MESH,
        ).wait_recv()
        return carry

    lax.fori_loop(1, n, wait_ids, 0)
    all_ids = ids_in[...]
    weight = jnp.zeros(all_ids.shape, jnp.float32)
    for doc in range(DOCS):
        hit = (all_ids == doc).astype(jnp.float32)
        count = jnp.sum(jnp.sum(hit, axis=2, keepdims=True), axis=0, keepdims=True)
        weight = weight + hit / jnp.maximum(count, 1.0)
    weights[...] = weight

    def turn(i, carry):
        group = lax.div(i, cores * (n // cores) // cores)
        j = i if cores == 1 else lax.rem(i, n // cores) * cores + lax.rem(c + group, cores)

        @pl.when(i >= n // cores)
        def _():
            wait_grad(j)

        row = weights[j]
        for first in range(0, panel, LANES):
            part = grads_in[token_rows(j), first : first + LANES].astype(jnp.float32)
            grads_t[first : first + LANES, token_rows(j)] = (part.T * row).astype(jnp.bfloat16)
        return carry

    lax.fori_loop(0, n, turn, 0)

    folds = panel // STRIDE
    per_tile = LANES // STRIDE
    tall = BLOCK // STRIDE
    tiles = panel // LANES
    row_sum = (
        lax.broadcasted_iota(jnp.int32, (folds, folds), 0) // tall
        == lax.broadcasted_iota(jnp.int32, (folds, folds), 1) // tall
    ).astype(jnp.float32)
    lane_sum = (
        lax.broadcasted_iota(jnp.int32, (width, width), 0) // BLOCK
        == lax.broadcasted_iota(jnp.int32, (width, width), 1) // BLOCK
    ).astype(jnp.float32)
    residue = (
        lax.broadcasted_iota(jnp.int32, (STRIDE, width), 0)
        + lax.broadcasted_iota(jnp.int32, (STRIDE, width), 1)
    ) % STRIDE

    def mask_of(q, tile):
        rows = []
        for a in range(tile * LANES // BLOCK, (tile + 1) * LANES // BLOCK):
            hit = residue == wide[q, a : a + 1, :]
            rows += [hit.astype(jnp.float32)] * tall
        return jnp.concatenate(rows, axis=0)

    def spread(values, mask):
        tall_values = jnp.broadcast_to(values[:, None, :], (per_tile, STRIDE, width))
        return tall_values.reshape(LANES, width) * mask

    def mix_rows(tile, values, way):
        both = dot32(tab_l[way], jnp.concatenate(split(values), axis=1))
        mixed = both[:LANES, :width] + (both[:LANES, width:] + both[LANES:, :width])
        high, low = split(mixed)
        mix[tile * LANES : (tile + 1) * LANES, :width] = high
        mix[tile * LANES : (tile + 1) * LANES, width:] = low

    def mix_columns(way):
        both = dot32(mix[...], tab_r[way])
        return both[:, :width] + both[:, width:]

    def invert(q, values):
        for tile in range(tiles):
            part = values[tile * per_tile : (tile + 1) * per_tile]
            mix_rows(tile, spread(part, mask_of(q, tile)), 1)
        return mix_columns(1)

    def out_copy(q, which):
        return pltpu.make_async_copy(
            (res_buf, upd_buf)[which].at[q],
            (res_out, upd_out)[which].at[:, pl.ds(pl.multiple_of(q * width, width), width)],
            o_sem.at[which, q],
        )

    def dec_copy(q, d):
        return pltpu.make_async_remote_copy(
            dec.at[q], dec_in.at[q, my_rep], d_send.at[q, d], d_recv.at[q, my_rep],
            device_id={"rep": lax.rem(my_rep + d, reps)}, device_id_type=MESH,
        )

    def finish_update(q):
        def wait_dec(d, inner):
            source = lax.rem(my_rep + d, reps)
            pltpu.make_async_remote_copy(
                dec.at[q], dec_in.at[q, source], d_send.at[q, d], d_recv.at[q, source],
                device_id={"rep": source}, device_id_type=MESH,
            ).wait_recv()
            return inner + dec_in[q, source]

        average = lax.fori_loop(1, reps, wait_dec, dec[q]) / reps
        upd_buf[q] = invert(q, average).astype(jnp.bfloat16)
        out_copy(q, 1).start()

    def first_half(q, carry):
        def wait_feat(d, inner):
            source = lax.rem(me + d, n)
            pltpu.make_async_remote_copy(
                feat.at[:, pl.ds(0, width)], cols_in.at[q, token_rows(source)],
                f_send.at[q, d], f_recv.at[q, source],
                device_id={"shard": source}, device_id_type=MESH,
            ).wait_recv()
            return inner

        lax.fori_loop(1, n, wait_feat, 0)
        lanes = pl.ds(pl.multiple_of(q * width, width), width)
        gradient = dot32(grads_t[...], cols_in[q]).astype(jnp.bfloat16).astype(jnp.float32)
        moment[...] = BETA * mom_in[:, lanes].astype(jnp.float32) + gradient
        for tile in range(tiles):
            mix_rows(tile, moment[tile * LANES : (tile + 1) * LANES, :], 0)
        spectrum = mix_columns(0)
        folded = []
        for tile in range(tiles):
            rows = slice(tile * LANES, (tile + 1) * LANES)
            chosen = (spectrum[rows] * mask_of(q, tile)).reshape(per_tile, STRIDE, width)
            folded.append(jnp.sum(chosen, axis=1))
        packed = jnp.concatenate(folded, axis=0)
        total = jnp.dot(row_sum, packed * packed, precision=PRECISE, preferred_element_type=jnp.float32)
        total = jnp.dot(total, lane_sum, precision=PRECISE, preferred_element_type=jnp.float32)
        mean_square = total / (BLOCK * tall)
        scale = (CLIP * jnp.sqrt(mean_square + EPS)).astype(jnp.bfloat16).astype(jnp.float32)
        quantized = jnp.clip(packed / scale, -1.0, 1.0).astype(jnp.bfloat16)
        decoded = quantized.astype(jnp.float32) * scale
        dec[q] = decoded

        def start_dec(d, inner):
            dec_copy(q, d).start()
            return inner

        lax.fori_loop(1, reps, start_dec, 0)
        res_buf[q] = (moment[...] - invert(q, decoded)).astype(jnp.bfloat16)
        out_copy(q, 0).start()

        @pl.when(q > 0)
        def _():
            finish_update(q - 1)

        return carry

    lax.fori_loop(0, chunks, first_half, 0)
    finish_update(chunks - 1)

    def drain(q, carry):
        def sent_feat(d, inner):
            feat_copy(q, d).wait_send()
            return inner

        def sent_dec(d, inner):
            dec_copy(q, d).wait_send()
            return inner

        lax.fori_loop(1, n, sent_feat, 0)
        lax.fori_loop(1, reps, sent_dec, 0)
        out_copy(q, 0).wait()
        out_copy(q, 1).wait()
        return carry

    def sent_ids(d, carry):
        ids_copy(d).wait_send()
        return carry

    lax.fori_loop(1, n, sent_ids, 0)
    for condition, j, slot, target, own in sends:

        @pl.when(condition)
        def _():
            grad_copy(j, slot, target, own).wait_send()

    lax.fori_loop(0, chunks, drain, 0)


def body(n, reps, features, out_grads, doc_ids, offsets, momentum):
    feat = features[0, 0]
    grads = out_grads[0, 0]
    tokens, model = feat.shape
    panel = grads.shape[1]
    row_width = momentum.shape[2]
    width = LANES
    chunks = row_width // width
    folds = panel // STRIDE
    anywhere = pl.BlockSpec(memory_space=pl.ANY)
    vmem = pl.BlockSpec(memory_space=pltpu.VMEM)
    dma = pltpu.SemaphoreType.DMA
    residual, update = pl.pallas_call(
        functools.partial(kernel, n, reps),
        out_shape=(
            jax.ShapeDtypeStruct((panel, row_width), jnp.bfloat16),
            jax.ShapeDtypeStruct((panel, row_width), jnp.bfloat16),
        ),
        in_specs=[anywhere, anywhere, vmem, vmem, anywhere, anywhere, anywhere],
        out_specs=(anywhere, anywhere),
        scratch_shapes=[
            pltpu.VMEM((chunks, n * tokens, width), jnp.bfloat16),
            pltpu.VMEM((n * tokens, panel), jnp.bfloat16),
            pltpu.VMEM((panel, n * tokens), jnp.bfloat16),
            pltpu.VMEM((n, 1, tokens), jnp.int32),
            pltpu.VMEM((n, 1, tokens), jnp.float32),
            pltpu.VMEM((panel, row_width), jnp.bfloat16),
            pltpu.VMEM((2, 2 * LANES, LANES), jnp.bfloat16),
            pltpu.VMEM((2, 2 * LANES, 2 * width), jnp.bfloat16),
            pltpu.VMEM((chunks, panel // BLOCK, width), jnp.int32),
            pltpu.VMEM((panel, width), jnp.float32),
            pltpu.VMEM((panel, 2 * width), jnp.bfloat16),
            pltpu.VMEM((chunks, folds, width), jnp.float32),
            pltpu.VMEM((chunks, reps, folds, width), jnp.float32),
            pltpu.VMEM((chunks, panel, width), jnp.bfloat16),
            pltpu.VMEM((chunks, panel, width), jnp.bfloat16),
            dma((5 + chunks,)),
            dma((n,)),
            dma((n,)),
            dma((n, 4)),
            dma((n,)),
            dma((chunks, n)),
            dma((chunks, n)),
            dma((chunks, reps)),
            dma((chunks, reps)),
            dma((2, chunks)),
        ],
        compiler_params=pltpu.CompilerParams(collective_id=0, has_side_effects=True),
    )(feat, grads, doc_ids[0], offsets[0].T, momentum[0], *map(jnp.asarray, dct_tables()))
    return residual[None], update[None]


def solution(mesh):
    return jax.shard_map(
        functools.partial(body, mesh.shape["shard"], mesh.shape["rep"]),
        mesh=mesh,
        in_specs=(
            P(None, "rep", "shard", None),
            P(None, "rep", "shard", None),
            P(None, "rep", "shard"),
            P(None, None, "shard"),
            P("rep", None, "shard"),
        ),
        out_specs=(P("rep", None, "shard"), P(None, None, "shard")),
        check_vma=False,
    )
```
